768 devices in a mesh: dp: 192 (over z, y, core), section: 4 (over x).
Axes of the slice: x: 4, y: 8, z: 12, core: 2. Of those that a mesh axis runs over, the one named last changes fastest.
Arguments:
- layer_inputs: bfloat16 [4, 24576, 4096], P('section', 'dp'), may hold values from -6 to 6
- top_grad: bfloat16 [24576, 4096], P('dp'), may hold values from -2.5 to 2.5
- value_grads: bfloat16 [4, 24576, 128], P('section', 'dp'), may hold values from -6 to 6
- weights: bfloat16 [4, 4096, 128], P('section'), may hold values from -0.09375 to 0.09375
- norm_gains: float32 [4, 4096], P('section'), may hold values from 0.5 to 1.5
- counts: int32 [1536], P('dp'), may hold values from 1 to 16, as said below
Outputs:
- input_grads: bfloat16 [4, 24576, 4096], P('section', 'dp')
- weight_grads: float32 [4, 528384], P('section', 'dp')
The draws below stay inside these ranges and needn't reach their ends.
Inputs may be any that keep to these rules, and one draw needn't show every extreme that they name: Entry m of a device's block of counts belongs to its m-th micro-batch; slots at or past the count are padding. Some micro-batch holds 16 live slots and some holds 1.
All inputs are finite; a program needn't handle non-finite values.
Results may differ from the reference program's by a relative error of at most 0.0034.
Values may be sent and summed in bfloat16 or wider, within the bound.
A program may use at most 32 MiB of HBM per device.

```python
import math
import jax
import jax.numpy as jnp
from jax import lax

D = 4096
R = 128
MB_ROWS = 16
MICRO = 8
SECTIONS = 4
TOKENS = 24576


def draw_counts(key, part):
    total = TOKENS // MB_ROWS
    key_list = jax.random.split(key, 4)
    device_level = jax.random.randint(key_list[0], (total // MICRO,), MB_ROWS // 2, MB_ROWS + 1)
    level = jnp.repeat(device_level, MICRO, total_repeat_length=total)
    raw_draw = jax.random.randint(key_list[1], (total,), 0, 1 << 20) % level + 1
    high_spot = jax.random.randint(key_list[2], (), 0, total)
    low_spot = (high_spot + 1 + jax.random.randint(key_list[3], (), 0, total - 1)) % total
    position = jnp.arange(total)
    raw_draw = jnp.where(position == high_spot, MB_ROWS, raw_draw)
    raw_draw = jnp.where(position == low_spot, 1, raw_draw)
    return raw_draw.astype(jnp.int32)


def block_scale(key, extent, shards, low, top_value):
    def one(dim, blocks):
        steps = jax.random.uniform(jax.random.fold_in(jax.random.fold_in(key, 6), dim), (blocks,), jnp.float32, low / len(shards), top_value / len(shards))
        return jnp.repeat(jnp.exp(steps), extent[dim] // blocks).reshape((-1,) + (1,) * (len(extent) - dim - 1))

    gain = one(*shards[0])
    for cut in shards[1:]:
        gain = gain * one(*cut)
    return gain


def centred(stream_key, shape, deviation, bound, pieces=(), kind=jnp.bfloat16):
    loudness = block_scale(stream_key, shape, pieces, -0.22, 0.18) if pieces else 1.0
    entries = jax.random.normal(stream_key, shape, jnp.float32) * deviation * loudness
    return jnp.minimum(jnp.maximum(entries, -bound), bound).astype(kind)


def setup_inputs(seed: int = 0) -> dict:
    streams_of = jax.random.split(jax.random.key(seed), 7)
    layer_inputs = centred(streams_of[0], (SECTIONS, TOKENS, D), 1.0, 6.0, ((0, 4), (1, 192)))
    top_grad = centred(streams_of[1], (TOKENS, D), 0.35, 2.5, ((0, 192),))
    value_grads = centred(streams_of[2], (SECTIONS, TOKENS, R), 1.0, 6.0, ((0, 4), (1, 192)))
    weights = centred(streams_of[3], (SECTIONS, D, R), D ** -0.5, 0.09375, ((0, 4),))
    norm_gains = jnp.clip(1.0 + 0.1 * jax.random.normal(streams_of[4], (SECTIONS, D), jnp.float32), 0.5, 1.5)
    counts = draw_counts(jax.random.fold_in(streams_of[6], 71), 0)
    return {"layer_inputs": layer_inputs, "top_grad": top_grad, "value_grads": value_grads, "weights": weights, "norm_gains": norm_gains, "counts": counts}


eps_norm = 1e-05

def reference(layer_inputs, top_grad, value_grads, weights, norm_gains, counts):
    slot_index = jnp.arange(MB_ROWS, dtype=jnp.int32)
    live = (slot_index[None, :] < counts[:, None]).reshape(TOKENS)
    factor = 1.0 / math.sqrt(TOKENS)
    carried = top_grad
    grads_list = [None] * SECTIONS
    packs_list = [None] * SECTIONS
    for layer in reversed(range(SECTIONS)):
        inputs_wide = layer_inputs[layer].astype(jnp.float32)
        scale = lax.rsqrt(lax.optimization_barrier(jnp.mean(inputs_wide * inputs_wide, axis=1, keepdims=True)) + eps_norm)
        unit = inputs_wide * scale
        gain_row = norm_gains[layer].astype(jnp.float32)
        normed = (unit * gain_row).astype(jnp.bfloat16)
        masked = jnp.where(live[:, None], value_grads[layer], jnp.zeros((), value_grads.dtype))
        back = lax.dot_general(masked, weights[layer], (((1,), (1,)), ((), ())), preferred_element_type=jnp.float32)
        branch = scale * (gain_row * back - unit * lax.optimization_barrier(jnp.mean(unit * gain_row * back, axis=1, keepdims=True)))
        carried = (carried.astype(jnp.float32) + branch).astype(jnp.bfloat16)
        grads_list[layer] = carried
        weight_term = lax.dot_general(normed, masked, (((0,), (0,)), ((), ())), preferred_element_type=jnp.float32)
        gain_term = lax.optimization_barrier(jnp.sum(unit * back, axis=0))
        packs_list[layer] = jnp.concatenate([gain_term, weight_term.reshape(-1)]) * factor
    return (jnp.stack(grads_list), jnp.stack(packs_list))
```

```python
import math

import jax
import jax.numpy as jnp
from jax import lax
from jax.experimental import pallas as pl
from jax.experimental.pallas import tpu as pltpu
from jax.sharding import PartitionSpec as P

EPS = 1e-05
MESH_ID = pl.DeviceIdType.MESH
F32, BF16 = jnp.float32, jnp.bfloat16

ROWS, WIDTH, VAL = 128, 4096, 128
MICRO, SLOTS = 8, 16
NZ, NY = 12, 8
BLOCK = 43
HALF = 24
ZROWS = NY * HALF

C1, C2 = 11 * 128, 22 * 128
STEP = 512


def pieces(low, high):
    return [(a, min(STEP, high - a)) for a in range(low, high, STEP)]


def kernel(
    counts, x_hbm, top_hbm, vg_hbm, w_hbm, g_hbm,
    out, owned,
    x, top, vg, w, g, br, nm, mk, ga, gx, gp, msg, rm, rp,
    pk, pf, zs, zr, ys, yr, rolled,
    lsem, ms, mr, ps, pr, xs, xr, zss, zrs, yss, yrs,
):
    dp = lax.axis_index("dp")
    sec = lax.axis_index("section")
    core = lax.rem(dp, 2)
    yy = lax.rem(lax.div(dp, 2), NY)
    zz = lax.div(dp, 2 * NY)

    def at(z, y, c):
        return (z * NY + y) * 2 + c

    behind = (dp, lax.rem(sec + 3, 4))
    ahead = (dp, lax.rem(sec + 1, 4))
    twin = (at(zz, yy, 1 - core), sec)
    zplus = (at(lax.rem(zz + 1, NZ), yy, core), sec)
    zminus = (at(lax.rem(zz + NZ - 1, NZ), yy, core), sec)
    yplus = (at(zz, lax.rem(yy + 1, NY), core), sec)
    yminus = (at(zz, lax.rem(yy + NY - 1, NY), core), sec)

    loads = [
        pltpu.make_async_copy(s, d, lsem.at[i])
        for i, (s, d) in enumerate(
            [(vg_hbm, vg), (w_hbm, w), (x_hbm, x), (g_hbm, g), (top_hbm, top)]
        )
    ]
    for cp in loads:
        cp.start()
    barrier = pltpu.get_barrier_semaphore()
    for peer in (behind, ahead, twin, zplus, zminus, yplus, yminus):
        pl.semaphore_signal(barrier, inc=1, device_id=peer, device_id_type=MESH_ID)

    def remote(src, dst, ssem, rsem, peer):
        return pltpu.make_async_remote_copy(
            src_ref=src, dst_ref=dst, send_sem=ssem, recv_sem=rsem,
            device_id=peer, device_id_type=MESH_ID,
        )

    def rows(k):
        return pl.ds(pl.multiple_of(k * SLOTS, SLOTS), SLOTS)

    def part(low, high):
        return pl.ds(low, high - low)

    def minus_cd(k, high):
        here = (rows(k), part(0, high))
        return remote(out.at[here], rm.at[here], ms.at[0, k], mr.at[0, k], behind)

    def minus_x(k):
        here = (rows(k), part(C2, WIDTH))
        return remote(msg.at[here], rm.at[here], ms.at[1, k], mr.at[1, k], behind)

    def plus_d(k):
        here = (rows(k), part(C1, C2))
        return remote(msg.at[here], rp.at[here], ps.at[0, k], pr.at[0, k], ahead)

    def plus_x(k, src):
        here = (rows(k), part(C2, WIDTH))
        return remote(src.at[here], rp.at[here], ps.at[1, k], pr.at[1, k], ahead)

    loads[0].wait()
    slot = lax.broadcasted_iota(jnp.int32, (SLOTS, VAL), 0)
    for m in range(MICRO):
        here = pl.ds(m * SLOTS, SLOTS)
        value = vg[here, :].astype(F32)
        mk[here, :] = jnp.where(slot < counts[0, m], value, 0.0).astype(BF16)
    loads[1].wait()
    for a in range(0, WIDTH, 1024):
        br[:, a : a + 1024] = lax.dot_general(
            mk[0:ROWS, :], w[a : a + 1024, :], (((1,), (1,)), ((), ())),
            preferred_element_type=F32,
        )
    loads[2].wait()
    loads[3].wait()
    loads[4].wait()
    ga[...] = jnp.zeros_like(ga)
    pl.semaphore_wait(barrier, 7)

    def first(k, carry):
        r = rows(k)
        square = jnp.zeros((SLOTS, 128), F32)
        cross = jnp.zeros((SLOTS, 128), F32)
        for a, n in pieces(0, WIDTH):
            xa = x[r, a : a + n].astype(F32)
            gb = g[0:1, a : a + n] * br[r, a : a + n]
            s2, c2 = xa * xa, xa * gb
            for j in range(0, n, 128):
                square = square + s2[:, j : j + 128]
                cross = cross + c2[:, j : j + 128]
        scale = lax.rsqrt(jnp.sum(square, axis=1, keepdims=True) * (1.0 / WIDTH) + EPS)
        mean = jnp.sum(cross, axis=1, keepdims=True) * scale * (1.0 / WIDTH)
        for a, n in pieces(0, WIDTH):
            cols = slice(a, a + n)
            unit = x[r, cols].astype(F32) * scale
            gr = g[0:1, cols]
            back = br[r, cols]
            nm[r, cols] = (unit * gr).astype(BF16)
            prod = unit * back
            ga[:, cols] += prod[0:8] + prod[8:16]
            br[r, cols] = scale * (gr * back - unit * mean)

        @pl.when(sec == 3)
        def _():
            for a, n in pieces(0, WIDTH):
                cols = slice(a, a + n)
                out[r, cols] = (top[r, cols].astype(F32) + br[r, cols]).astype(BF16)
            minus_cd(k, C2).start()

        @pl.when(sec == 1)
        def _():
            for a, n in pieces(C1, WIDTH):
                msg[r, a : a + n] = br[r, a : a + n].astype(BF16)
            plus_d(k).start()
            minus_x(k).start()

        @pl.when(sec == 2)
        def _():
            for a, n in pieces(C2, WIDTH):
                msg[r, a : a + n] = br[r, a : a + n].astype(BF16)
            plus_x(k, msg).start()

        return carry

    lax.fori_loop(0, MICRO, first, 0)

    for j in range(WIDTH // 128):
        gx[j : j + 1, :] = jnp.sum(ga[:, j * 128 : j * 128 + 128], axis=0, keepdims=True)
    swaps = [
        remote(nm.at[pl.ds(0, ROWS)], nm.at[pl.ds(ROWS, ROWS)], xs.at[0], xr.at[0], twin),
        remote(mk.at[pl.ds(0, ROWS)], mk.at[pl.ds(ROWS, ROWS)], xs.at[1], xr.at[1], twin),
        remote(gx, gp, xs.at[2], xr.at[2], twin),
    ]
    for cp in swaps:
        cp.start()

    def node3_d(k):
        plus_d(k).wait_recv()
        r = rows(k)
        for a, n in pieces(C1, C2):
            msg[r, a : a + n] = (rp[r, a : a + n].astype(F32) + br[r, a : a + n]).astype(BF16)
        plus_d(k).start()

    def node3_x(k):
        plus_x(k, msg).wait_recv()
        r = rows(k)
        for a, n in pieces(C2, WIDTH):
            msg[r, a : a + n] = (rp[r, a : a + n].astype(F32) + br[r, a : a + n]).astype(BF16)
        plus_x(k, msg).start()

    def node2_cd(k):
        minus_cd(k, C2).wait_recv()
        r = rows(k)
        for a, n in pieces(0, C2):
            out[r, a : a + n] = (rm[r, a : a + n].astype(F32) + br[r, a : a + n]).astype(BF16)
        minus_cd(k, C2).start()

    def node2_x(k):
        plus_x(k, msg).wait_recv()
        r = rows(k)
        for a, n in pieces(C2, WIDTH):
            out[r, a : a + n] = (
                top[r, a : a + n].astype(F32) + rp[r, a : a + n].astype(F32)
            ).astype(BF16)

    def node1_cd(k):
        minus_cd(k, C2).wait_recv()
        r = rows(k)
        for a, n in pieces(0, C1):
            out[r, a : a + n] = (rm[r, a : a + n].astype(F32) + br[r, a : a + n]).astype(BF16)
        minus_cd(k, C1).start()
        for a, n in pieces(C1, C2):
            out[r, a : a + n] = (rm[r, a : a + n].astype(F32) + br[r, a : a + n]).astype(BF16)

    def node1_x(k):
        plus_x(k, rp).wait_recv()
        plus_x(k, rp).start()
        r = rows(k)
        for a, n in pieces(C2, WIDTH):
            total = top[r, a : a + n].astype(F32) + rp[r, a : a + n].astype(F32)
            out[r, a : a + n] = (total + br[r, a : a + n]).astype(BF16)

    def node0_x_forward(k):
        plus_x(k, rp).wait_recv()
        plus_x(k, rp).start()

    def node0_x(k):
        minus_x(k).wait_recv()
        r = rows(k)
        for a, n in pieces(C2, WIDTH):
            total = top[r, a : a + n].astype(F32) + rp[r, a : a + n].astype(F32)
            total = total + rm[r, a : a + n].astype(F32)
            out[r, a : a + n] = (total + br[r, a : a + n]).astype(BF16)

    def node0_d(k):
        plus_d(k).wait_recv()
        r = rows(k)
        for a, n in pieces(C1, C2):
            total = top[r, a : a + n].astype(F32) + rp[r, a : a + n].astype(F32)
            out[r, a : a + n] = (total + br[r, a : a + n]).astype(BF16)

    def node0_c(k):
        minus_cd(k, C1).wait_recv()
        r = rows(k)
        for a, n in pieces(0, C1):
            out[r, a : a + n] = (rm[r, a : a + n].astype(F32) + br[r, a : a + n]).astype(BF16)

    script = [
        (3, node3_x, 0), (3, node3_d, 0),
        (2, node3_d, 0), (2, node2_cd, 0), (2, node2_x, 3),
        (1, node1_cd, 0), (1, node1_x, 1),
        (0, node0_x_forward, 0), (0, node0_x, 1), (0, node0_d, 1), (0, node0_c, 2),
    ]

    def chain(i):
        for section in range(4):
            todo = [
                (step, i - lag) for s, step, lag in script
                if s == section and 0 <= i - lag < MICRO
            ]
            if not todo:
                continue

            @pl.when(sec == section)
            def _(todo=todo):
                for step, k in todo:
                    step(k)

    def z_copy(i, peer):
        return remote(zs.at[i], zr.at[i], zss.at[i], zrs.at[i], peer)

    def z_step(s):
        up = pf[lax.rem(zz + 6 - s, NZ)]
        if s > 0:
            z_copy(s - 1, zplus).wait_recv()
            up = up + zr[s - 1].astype(F32)
        zs[s] = up.astype(BF16)
        z_copy(s, zplus).start()
        if s < 5:
            down = pf[lax.rem(zz + NZ - 5 + s, NZ)]
            if s > 0:
                z_copy(6 + s - 1, zminus).wait_recv()
                down = down + zr[6 + s - 1].astype(F32)
            zs[6 + s] = down.astype(BF16)
            z_copy(6 + s, zminus).start()

    def z_last():
        z_copy(5, zplus).wait_recv()
        z_copy(10, zminus).wait_recv()
        pf[zz] = pf[zz] + zr[5].astype(F32) + zr[10].astype(F32)

    def y_own(y):
        return pf[zz, pl.ds(pl.multiple_of(y * HALF, 8), HALF), :]

    def y_copy(i, peer):
        return remote(ys.at[i], yr.at[i], yss.at[i], yrs.at[i], peer)

    def y_step(s):
        up = y_own(lax.rem(yy + 4 - s, NY))
        if s > 0:
            y_copy(s - 1, yplus).wait_recv()
            up = up + yr[s - 1]
        ys[s] = up
        y_copy(s, yplus).start()
        if s < 3:
            down = y_own(lax.rem(yy + NY - 3 + s, NY))
            if s > 0:
                y_copy(4 + s - 1, yminus).wait_recv()
                down = down + yr[4 + s - 1]
            ys[4 + s] = down
            y_copy(4 + s, yminus).start()

    def y_last():
        y_copy(3, yplus).wait_recv()
        y_copy(6, yminus).wait_recv()
        total = (y_own(yy) + yr[3] + yr[6]) * (1.0 / math.sqrt(ROWS * 2 * NY * NZ))
        rolled[0:HALF, :] = pltpu.roll(total, 64, 1)
        lane = lax.broadcasted_iota(jnp.int32, (HALF, 128), 1)
        late = jnp.where(lane < 64, rolled[0:HALF, :], rolled[1 : HALF + 1, :])
        mine = jnp.where(core == 1, late, total)
        for j in range(21):
            owned[0:1, j * 128 : j * 128 + 128] = mine[j : j + 1, :]
        owned[0:1, 2688:2752] = mine[21:22, 0:64]

    for cp in swaps:
        cp.wait()
    pk[0:32, :] = gx[...] + gp[...]
    for a in range(0, WIDTH, 512):
        pk[32 + a : 32 + a + 512, :] = lax.dot_general(
            nm[:, a : a + 512], mk[...], (((0,), (0,)), ((), ())),
            preferred_element_type=F32,
        )

    def pack(z, carry):
        for y in range(NY):
            start = z * (NY * BLOCK) + y * BLOCK + core * 21
            pf[z, y * HALF : y * HALF + HALF, :] = pk[pl.ds(start, HALF), :]
        return carry

    pk[4128:4136, :] = jnp.zeros((8, 128), F32)
    lax.fori_loop(0, NZ, pack, 0)

    z_step(0)
    chain(0)
    for i in range(1, 6):
        z_step(i)
        chain(i)
    z_last()
    y_step(0)
    chain(6)
    y_step(1)
    chain(7)
    y_step(2)
    chain(8)
    y_step(3)
    chain(9)
    y_last()
    chain(10)

    for i in range(11):
        z_copy(i, zplus).wait_send()
    for i in range(7):
        y_copy(i, yplus).wait_send()

    def drain(k, carry):
        @pl.when(sec >= 2)
        def _():
            minus_cd(k, C2).wait_send()

        @pl.when(sec == 1)
        def _():
            minus_cd(k, C1).wait_send()
            minus_x(k).wait_send()

        @pl.when(sec >= 1)
        def _():
            plus_d(k).wait_send()

        plus_x(k, msg).wait_send()
        return carry

    lax.fori_loop(0, MICRO, drain, 0)


def shards(layer_inputs, top_grad, value_grads, weights, norm_gains, counts):
    anywhere = pl.BlockSpec(memory_space=pl.ANY)
    local = pl.BlockSpec(memory_space=pltpu.VMEM)
    dma = pltpu.SemaphoreType.DMA
    wide = (ROWS, WIDTH)
    grads, owned = pl.pallas_call(
        kernel,
        out_shape=(
            jax.ShapeDtypeStruct(wide, BF16),
            jax.ShapeDtypeStruct((1, 2752), F32),
        ),
        in_specs=[pl.BlockSpec(memory_space=pltpu.SMEM)] + [anywhere] * 5,
        out_specs=(local, local),
        scratch_shapes=[
            pltpu.VMEM(wide, BF16),
            pltpu.VMEM(wide, BF16),
            pltpu.VMEM((ROWS, VAL), BF16),
            pltpu.VMEM((WIDTH, VAL), BF16),
            pltpu.VMEM((1, WIDTH), F32),
            pltpu.VMEM(wide, F32),
            pltpu.VMEM((2 * ROWS, WIDTH), BF16),
            pltpu.VMEM((2 * ROWS, VAL), BF16),
            pltpu.VMEM((8, WIDTH), F32),
            pltpu.VMEM((32, 128), F32),
            pltpu.VMEM((32, 128), F32),
            pltpu.VMEM(wide, BF16),
            pltpu.VMEM(wide, BF16),
            pltpu.VMEM(wide, BF16),
            pltpu.VMEM((4136, 128), F32),
            pltpu.VMEM((NZ, ZROWS, 128), F32),
            pltpu.VMEM((11, ZROWS, 128), BF16),
            pltpu.VMEM((11, ZROWS, 128), BF16),
            pltpu.VMEM((7, HALF, 128), F32),
            pltpu.VMEM((7, HALF, 128), F32),
            pltpu.VMEM((HALF + 8, 128), F32),
            dma((5,)),
            dma((2, MICRO)), dma((2, MICRO)), dma((2, MICRO)), dma((2, MICRO)),
            dma((3,)), dma((3,)),
            dma((11,)), dma((11,)), dma((7,)), dma((7,)),
        ],
        compiler_params=pltpu.CompilerParams(
            collective_id=0, has_side_effects=True, vmem_limit_bytes=40 * 2**20
        ),
    )(
        counts.reshape(1, MICRO), layer_inputs[0], top_grad, value_grads[0],
        weights[0], norm_gains,
    )
    return grads.reshape(1, ROWS, WIDTH), owned


def solution(mesh):
    placed = (
        P("section", "dp", None),
        P("dp", None),
        P("section", "dp", None),
        P("section", None, None),
        P("section", None),
        P("dp"),
    )
    return jax.shard_map(
        shards,
        mesh=mesh,
        in_specs=placed,
        out_specs=(P("section", "dp", None), P("section", "dp")),
        check_vma=False,
    )
```

```python
import math

import jax
import jax.numpy as jnp
from jax import lax
from jax.experimental import pallas as pl
from jax.experimental.pallas import tpu as pltpu
from jax.sharding import PartitionSpec as P

EPS = 1e-05
MESH_ID = pl.DeviceIdType.MESH
F32, BF16 = jnp.float32, jnp.bfloat16

ROWS, WIDTH, VAL = 128, 4096, 128
MICRO, SLOTS = 8, 16
NZ, NY = 12, 8
BLOCK = 43
HALF = 24
PAIR = 2 * HALF
GROUPS = ((0, 2), (2, 6), (6, 12))

C1, C2 = 11 * 128, 22 * 128
STEP = 512

ORDER = (
    (
        (),
        (("b", 0),),
        (("c", 0),),
        (("x", 0),),
    ),
    (
        (("xf", 0), ("x", 0), ("xf", 1), ("x", 1), ("c", 0), ("xf", 2), ("x", 2), ("xf", 3), ("xf", 4), ("c", 1), ("xf", 5), ("x", 3)),
        (("b", 1), ("c", 0), ("b", 2), ("c", 1), ("b", 3), ("x", 0), ("c", 2), ("c", 3), ("b", 4), ("x", 1), ("c", 4), ("x", 2)),
        (("c", 1), ("c", 2), ("d", 0), ("d", 1), ("d", 2), ("c", 3), ("d", 3), ("c", 4), ("d", 4), ("c", 5), ("d", 5), ("c", 6), ("d", 6), ("c", 7), ("d", 7), ("e", 0), ("x", 0), ("e", 1)),
        (("x", 1), ("x", 2), ("x", 3), ("x", 4), ("x", 5), ("x", 6), ("x", 7), ("d", 0), ("d", 1)),
    ),
    (
        (("xf", 6), ("c", 2), ("xf", 7), ("c", 3), ("d", 0), ("x", 4), ("d", 1)),
        (("c", 5), ("b", 5), ("x", 3), ("c", 6), ("x", 4), ("c", 7), ("b", 6), ("x", 5), ("e", 0), ("x", 6)),
        (("e", 2), ("x", 1), ("e", 3), ("x", 2), ("e", 4), ("x", 3)),
        (("d", 2), ("d", 3), ("d", 4), ("d", 5)),
    ),
    (
        (("c", 4), ("d", 2), ("c", 5), ("d", 3), ("x", 5), ("d", 4), ("c", 6), ("d", 5), ("c", 7), ("d", 6), ("x", 6)),
        (("e", 1), ("x", 7), ("b", 7), ("e", 2), ("e", 3), ("e", 4), ("e", 5), ("e", 6)),
        (("e", 5), ("x", 4), ("e", 6), ("x", 5), ("e", 7), ("x", 6), ("x", 7)),
        (("d", 6), ("d", 7)),
    ),
    (
        (("d", 7), ("x", 7)),
        (("e", 7),),
        (),
        (),
    ),
)


def pieces(low, high):
    return [(a, min(STEP, high - a)) for a in range(low, high, STEP)]


def kernel(
    counts, x_hbm, top_hbm, vg_hbm, w_hbm, g_hbm,
    out, owned,
    x, top, vg, w, g, br, nm, mk, ga, gx, gp, msg, rm, rp,
    pk, zs, zr, ys, yr, half, rolled,
    lsem, ms, mr, ps, pr, xs, xr, zss, zrs, yss, yrs, hs, hr, hello,
):
    dp = lax.axis_index("dp")
    sec = lax.axis_index("section")
    core = lax.rem(dp, 2)
    yy = lax.rem(lax.div(dp, 2), NY)
    zz = lax.div(dp, 2 * NY)

    def at(z, y, c):
        return (z * NY + y) * 2 + c

    behind = (dp, lax.rem(sec + 3, 4))
    ahead = (dp, lax.rem(sec + 1, 4))
    twin = (at(zz, yy, 1 - core), sec)
    lead = core == 0

    def on_y(d):
        return (at(zz, lax.rem(yy + d, NY), 0), sec)

    def on_z(d):
        return (at(lax.rem(zz + d, NZ), yy, 0), sec)

    loads = [
        pltpu.make_async_copy(s, d, lsem.at[i])
        for i, (s, d) in enumerate(
            [(vg_hbm, vg), (w_hbm, w), (x_hbm, x), (g_hbm, g), (top_hbm, top)]
        )
    ]
    for cp in loads:
        cp.start()
    barrier = pltpu.get_barrier_semaphore()
    def signal(sem, peer):
        pl.semaphore_signal(sem, inc=1, device_id=peer, device_id_type=MESH_ID)

    signal(barrier, behind)
    signal(barrier, ahead)

    @pl.when(lead)
    def _():
        signal(barrier, twin)
        for d in range(1, NY):
            pl.when(yy + d < NY)(lambda d=d: signal(barrier, on_y(d)))
        for d in range(1, NZ):
            pl.when(zz + d < NZ)(lambda d=d: signal(barrier, on_z(d)))

    def remote(src, dst, ssem, rsem, peer):
        return pltpu.make_async_remote_copy(
            src_ref=src, dst_ref=dst, send_sem=ssem, recv_sem=rsem,
            device_id=peer, device_id_type=MESH_ID,
        )

    def rows(k):
        return pl.ds(pl.multiple_of(k * SLOTS, SLOTS), SLOTS)

    def part(low, high):
        return pl.ds(low, high - low)

    def minus_c(k):
        here = (rows(k), part(0, C1))
        return remote(out.at[here], rm.at[here], ms.at[0, k], mr.at[0, k], behind)

    def minus_d(k):
        here = (rows(k), part(C1, C2))
        return remote(out.at[here], rm.at[here], ms.at[2, k], mr.at[2, k], behind)

    def minus_x(k):
        here = (rows(k), part(C2, WIDTH))
        return remote(msg.at[here], rm.at[here], ms.at[1, k], mr.at[1, k], behind)

    def plus_d(k):
        here = (rows(k), part(C1, C2))
        return remote(msg.at[here], rp.at[here], ps.at[0, k], pr.at[0, k], ahead)

    def plus_x(k, src):
        here = (rows(k), part(C2, WIDTH))
        return remote(src.at[here], rp.at[here], ps.at[1, k], pr.at[1, k], ahead)

    loads[0].wait()
    slot = lax.broadcasted_iota(jnp.int32, (SLOTS, VAL), 0)
    for m in range(MICRO):
        here = pl.ds(m * SLOTS, SLOTS)
        value = vg[here, :].astype(F32)
        mk[here, :] = jnp.where(slot < counts[0, m], value, 0.0).astype(BF16)
    loads[1].wait()
    for a in range(0, WIDTH, 1024):
        br[:, a : a + 1024] = lax.dot_general(
            mk[0:ROWS, :], w[a : a + 1024, :], (((1,), (1,)), ((), ())),
            preferred_element_type=F32,
        )
    loads[2].wait()
    loads[3].wait()
    loads[4].wait()
    ga[...] = jnp.zeros_like(ga)
    pl.semaphore_wait(barrier, jnp.where(lead, 2 + yy + zz, 3))

    @pl.when(lead)
    def _():
        for d in range(1, NY):
            pl.when(yy + d >= NY)(lambda d=d: signal(hello.at[0], on_y(d)))
        for d in range(1, NZ):
            pl.when(zz + d >= NZ)(lambda d=d: signal(hello.at[1], on_z(d)))

    def swap_rows(k):
        there = pl.ds(pl.multiple_of(ROWS + k * SLOTS, SLOTS), SLOTS)
        return remote(nm.at[rows(k)], nm.at[there], xs.at[k], xr.at[k], twin)


    def first(k, carry):
        r = rows(k)
        square = jnp.zeros((SLOTS, 128), F32)
        cross = jnp.zeros((SLOTS, 128), F32)
        for a, n in pieces(0, WIDTH):
            xa = x[r, a : a + n].astype(F32)
            gb = g[0:1, a : a + n] * br[r, a : a + n]
            s2, c2 = xa * xa, xa * gb
            for j in range(0, n, 128):
                square = square + s2[:, j : j + 128]
                cross = cross + c2[:, j : j + 128]
        scale = lax.rsqrt(jnp.sum(square, axis=1, keepdims=True) * (1.0 / WIDTH) + EPS)
        mean = jnp.sum(cross, axis=1, keepdims=True) * scale * (1.0 / WIDTH)
        for a, n in pieces(0, WIDTH):
            cols = slice(a, a + n)
            unit = x[r, cols].astype(F32) * scale
            gr = g[0:1, cols]
            back = br[r, cols]
            nm[r, cols] = (unit * gr).astype(BF16)
            prod = unit * back
            ga[:, cols] += prod[0:8] + prod[8:16]
            br[r, cols] = scale * (gr * back - unit * mean)

        pl.when(core == 1)(lambda: swap_rows(k).start())

        @pl.when(sec == 3)
        def _():
            for a, n in pieces(0, WIDTH):
                cols = slice(a, a + n)
                out[r, cols] = (top[r, cols].astype(F32) + br[r, cols]).astype(BF16)
            minus_c(k).start()

        @pl.when(sec == 1)
        def _():
            for a, n in pieces(C1, WIDTH):
                msg[r, a : a + n] = br[r, a : a + n].astype(BF16)
            plus_d(k).start()

        @pl.when(sec == 2)
        def _():
            for a, n in pieces(C2, WIDTH):
                msg[r, a : a + n] = br[r, a : a + n].astype(BF16)
            plus_x(k, msg).start()

        return carry

    lax.fori_loop(0, MICRO, first, 0)

    @pl.when(sec == 3)
    def _():
        for k in range(MICRO):
            minus_d(k).start()

    for j in range(WIDTH // 128):
        gx[j : j + 1, :] = jnp.sum(ga[:, j * 128 : j * 128 + 128], axis=0, keepdims=True)
    swaps = [
        remote(mk.at[pl.ds(0, ROWS)], mk.at[pl.ds(ROWS, ROWS)], xs.at[8], xr.at[8], twin),
        remote(gx, gp, xs.at[9], xr.at[9], twin),
    ]

    @pl.when(core == 1)
    def _():
        for cp in swaps:
            cp.start()

    def node3_d(k):
        plus_d(k).wait_recv()
        r = rows(k)
        for a, n in pieces(C1, C2):
            msg[r, a : a + n] = (rp[r, a : a + n].astype(F32) + br[r, a : a + n]).astype(BF16)
        plus_d(k).start()

    def node3_x(k):
        plus_x(k, msg).wait_recv()
        r = rows(k)
        for a, n in pieces(C2, WIDTH):
            msg[r, a : a + n] = (rp[r, a : a + n].astype(F32) + br[r, a : a + n]).astype(BF16)
        plus_x(k, msg).start()

    def add_minus(k, low, high):
        r = rows(k)
        for a, n in pieces(low, high):
            out[r, a : a + n] = (rm[r, a : a + n].astype(F32) + br[r, a : a + n]).astype(BF16)

    def relay_c(k):
        minus_c(k).wait_recv()
        add_minus(k, 0, C1)
        minus_c(k).start()

    def node2_e(k):
        minus_d(k).wait_recv()
        add_minus(k, C1, C2)
        minus_d(k).start()

    def node2_x(k):
        plus_x(k, msg).wait_recv()
        r = rows(k)
        for a, n in pieces(C2, WIDTH):
            out[r, a : a + n] = (
                top[r, a : a + n].astype(F32) + rp[r, a : a + n].astype(F32)
            ).astype(BF16)

    def node1_e(k):
        minus_d(k).wait_recv()
        add_minus(k, C1, C2)

    def node1_b(k):
        minus_x(k).start()

    def node1_x(k):
        plus_x(k, rp).wait_recv()
        plus_x(k, rp).start()
        r = rows(k)
        for a, n in pieces(C2, WIDTH):
            total = top[r, a : a + n].astype(F32) + rp[r, a : a + n].astype(F32)
            out[r, a : a + n] = (total + br[r, a : a + n]).astype(BF16)

    def node0_x_forward(k):
        plus_x(k, rp).wait_recv()
        plus_x(k, rp).start()

    def node0_x(k):
        minus_x(k).wait_recv()
        r = rows(k)
        for a, n in pieces(C2, WIDTH):
            total = top[r, a : a + n].astype(F32) + rp[r, a : a + n].astype(F32)
            total = total + rm[r, a : a + n].astype(F32)
            out[r, a : a + n] = (total + br[r, a : a + n]).astype(BF16)

    def node0_d(k):
        plus_d(k).wait_recv()
        r = rows(k)
        for a, n in pieces(C1, C2):
            total = top[r, a : a + n].astype(F32) + rp[r, a : a + n].astype(F32)
            out[r, a : a + n] = (total + br[r, a : a + n]).astype(BF16)

    def node0_c(k):
        minus_c(k).wait_recv()
        add_minus(k, 0, C1)

    steps = (
        {"xf": node0_x_forward, "x": node0_x, "d": node0_d, "c": node0_c},
        {"b": node1_b, "c": relay_c, "e": node1_e, "x": node1_x},
        {"c": relay_c, "d": node3_d, "e": node2_e, "x": node2_x},
        {"x": node3_x, "d": node3_d},
    )

    def chain(stretch):
        for section in range(4):
            todo = ORDER[stretch][section]
            if not todo:
                continue

            @pl.when(sec == section)
            def _(section=section, todo=todo):
                for name, k in todo:
                    steps[section][name](k)

    def owner_rows(z, y):
        start = z * (NY * BLOCK) + y * BLOCK
        return jnp.concatenate([pk[pl.ds(start, HALF), :], pk[pl.ds(start + 21, HALF), :]], axis=0)

    def group_rows(group):
        return pl.ds(group[0] * PAIR, (group[1] - group[0]) * PAIR)

    def y_copy(d, i):
        there = group_rows(GROUPS[i])
        return remote(
            ys.at[lax.rem(yy + d, NY), there], yr.at[NY - d, there],
            yss.at[d, i], yrs.at[NY - d, i], on_y(d),
        )

    def z_copy(z):
        return remote(zs.at[z], zr.at[zz], zss.at[z], zrs.at[zz], (at(z, yy, 0), sec))

    def product():
        for k in range(MICRO):
            swap_rows(k).wait_recv()
        for cp in swaps:
            cp.wait_recv()
        pk[0:32, :] = gx[...] + gp[...]
        for a in range(0, WIDTH, 512):
            pk[32 + a : 32 + a + 512, :] = lax.dot_general(
                nm[:, a : a + 512], mk[...], (((0,), (0,)), ((), ())),
                preferred_element_type=F32,
            )
        pk[4128:4136, :] = jnp.zeros((8, 128), F32)
        pl.when(yy < NY - 1)(lambda: pl.semaphore_wait(hello.at[0], NY - 1 - yy))
        for i, group in enumerate(GROUPS):
            def pack(z, carry):
                for y in range(NY):
                    here = pl.ds(pl.multiple_of(z * PAIR, PAIR), PAIR)
                    ys[y, here, :] = owner_rows(z, y).astype(BF16)
                return carry

            lax.fori_loop(group[0], group[1], pack, 0)
            for d in (4, 3, 5, 2, 6, 1, 7):
                y_copy(d, i).start()

    def y_sum(i):
        low, high = GROUPS[i]
        for d in range(1, NY):
            y_copy(NY - d, i).wait_recv()

        def add(z, carry):
            here = pl.ds(pl.multiple_of(z * PAIR, PAIR), PAIR)
            total = owner_rows(z, yy)
            for d in range(1, NY):
                total = total + yr[d, here, :].astype(F32)
            half[z] = total
            zs[z] = total.astype(BF16)
            return carry

        lax.fori_loop(low, high, add, 0)
        if i == 0:
            zr[zz] = jnp.zeros((PAIR, 128), BF16)
            pl.when(zz < NZ - 1)(lambda: pl.semaphore_wait(hello.at[1], NZ - 1 - zz))
        for z in range(low, high):
            pl.when(zz != z)(lambda z=z: z_copy(z).start())

    def z_arrival(z):
        return remote(zs.at[z], zr.at[z], zss.at[z], zrs.at[z], (at(z, yy, 0), sec))

    give = remote(rolled.at[1], rolled.at[2], hs, hr, twin)
    factor = 1.0 / math.sqrt(ROWS * 2 * NY * NZ)

    def z_sum():
        for z in range(NZ):
            pl.when(zz != z)(lambda z=z: z_arrival(z).wait_recv())
        total = half[zz]
        for z in range(NZ):
            total = total + zr[z].astype(F32)
        total = total * factor
        rolled[1] = total[HALF:PAIR]
        give.start()
        for j in range(21):
            owned[0:1, j * 128 : j * 128 + 128] = total[j : j + 1, :]
        owned[0:1, 2688:2752] = total[21:22, 0:64]

    def twin_last():
        give.wait_recv()
        turned = pltpu.roll(rolled[2], 64, 1)
        rolled[0] = turned
        lane = lax.broadcasted_iota(jnp.int32, (22, 128), 1)
        mine = jnp.where(lane < 64, rolled[0, 0:22, :], rolled[0, 1:23, :])
        for j in range(21):
            owned[0:1, j * 128 : j * 128 + 128] = mine[j : j + 1, :]
        owned[0:1, 2688:2752] = mine[21:22, 0:64]

    chain(0)
    pl.when(lead)(product)
    chain(1)
    pl.when(lead)(lambda: y_sum(0))
    chain(2)
    pl.when(lead)(lambda: y_sum(1))
    chain(3)
    pl.when(lead)(lambda: y_sum(2))
    chain(4)
    pl.when(lead)(z_sum)
    pl.when(core == 1)(twin_last)

    @pl.when(lead)
    def _():
        for i in range(len(GROUPS)):
            for d in range(1, NY):
                y_copy(d, i).wait_send()
        for z in range(NZ):
            pl.when(zz != z)(lambda z=z: z_copy(z).wait_send())
        give.wait_send()

    @pl.when(core == 1)
    def _():
        for k in range(MICRO):
            swap_rows(k).wait_send()
        for cp in swaps:
            cp.wait_send()

    def drain(k, carry):
        @pl.when(sec >= 2)
        def _():
            minus_d(k).wait_send()

        @pl.when(sec == 1)
        def _():
            minus_x(k).wait_send()

        @pl.when(sec >= 1)
        def _():
            minus_c(k).wait_send()
            plus_d(k).wait_send()

        plus_x(k, msg).wait_send()
        return carry

    lax.fori_loop(0, MICRO, drain, 0)


def shards(layer_inputs, top_grad, value_grads, weights, norm_gains, counts):
    anywhere = pl.BlockSpec(memory_space=pltpu.HBM)
    local = pl.BlockSpec(memory_space=pltpu.VMEM)
    dma = pltpu.SemaphoreType.DMA
    wide = (ROWS, WIDTH)
    grads, owned = pl.pallas_call(
        kernel,
        out_shape=(
            jax.ShapeDtypeStruct(wide, BF16),
            jax.ShapeDtypeStruct((1, 2752), F32),
        ),
        in_specs=[pl.BlockSpec(memory_space=pltpu.SMEM)] + [anywhere] * 5,
        out_specs=(local, local),
        scratch_shapes=[
            pltpu.VMEM(wide, BF16),
            pltpu.VMEM(wide, BF16),
            pltpu.VMEM((ROWS, VAL), BF16),
            pltpu.VMEM((WIDTH, VAL), BF16),
            pltpu.VMEM((1, WIDTH), F32),
            pltpu.VMEM(wide, F32),
            pltpu.VMEM((2 * ROWS, WIDTH), BF16),
            pltpu.VMEM((2 * ROWS, VAL), BF16),
            pltpu.VMEM((8, WIDTH), F32),
            pltpu.VMEM((32, 128), F32),
            pltpu.VMEM((32, 128), F32),
            pltpu.VMEM(wide, BF16),
            pltpu.VMEM(wide, BF16),
            pltpu.VMEM(wide, BF16),
            pltpu.VMEM((4136, 128), F32),
            pltpu.VMEM((NZ, PAIR, 128), BF16),
            pltpu.VMEM((NZ, PAIR, 128), BF16),
            pltpu.VMEM((NY, NZ * PAIR, 128), BF16),
            pltpu.VMEM((NY, NZ * PAIR, 128), BF16),
            pltpu.VMEM((NZ, PAIR, 128), F32),
            pltpu.VMEM((3, HALF, 128), F32),
            dma((5,)),
            dma((3, MICRO)), dma((3, MICRO)), dma((2, MICRO)), dma((2, MICRO)),
            dma((10,)), dma((10,)),
            dma((NZ,)), dma((NZ,)),
            dma((NY, len(GROUPS))), dma((NY, len(GROUPS))),
            dma, dma,
            pltpu.SemaphoreType.REGULAR((2,)),
        ],
        compiler_params=pltpu.CompilerParams(
            collective_id=0, has_side_effects=True, vmem_limit_bytes=62 * 2**20
        ),
    )(
        counts.reshape(1, MICRO), layer_inputs[0], top_grad, value_grads[0],
        weights[0], norm_gains,
    )
    return grads.reshape(1, ROWS, WIDTH), owned


def solution(mesh):
    placed = (
        P("section", "dp", None),
        P("dp", None),
        P("section", "dp", None),
        P("section", None, None),
        P("section", None),
        P("dp"),
    )
    return jax.shard_map(
        shards,
        mesh=mesh,
        in_specs=placed,
        out_specs=(P("section", "dp", None), P("section", "dp")),
        check_vma=False,
    )
```

```python
import math

import jax
import jax.numpy as jnp
from jax import lax
from jax.experimental import pallas as pl
from jax.experimental.pallas import tpu as pltpu
from jax.sharding import PartitionSpec as P

EPS = 1e-05
MESH_ID = pl.DeviceIdType.MESH
F32, BF16 = jnp.float32, jnp.bfloat16

ROWS, WIDTH, VAL = 128, 4096, 128
MICRO, SLOTS = 8, 16
NZ, NY = 12, 8
BLOCK = 43
HALF = 24
PAIR = 2 * HALF
GROUPS = ((0, 2), (2, 5), (5, 8), (8, 12))

C1, C2 = 11 * 128, 22 * 128
STEP = 512

ORDER = (
    (
        (),
        (("b", 0),),
        (),
        (),
    ),
    (
        (("xf", 0),),
        (("b", 1), ("b", 2), ("c", 0), ("b", 3), ("c", 1), ("c", 2)),
        (("c", 0), ("d", 0), ("c", 1), ("d", 1), ("c", 2), ("d", 2), ("c", 3), ("d", 3), ("c", 4), ("d", 4), ("c", 5), ("d", 5)),
        (("x", 0), ("x", 1), ("x", 2), ("x", 3), ("x", 4), ("x", 5), ("x", 6), ("x", 7)),
    ),
    (
        (("xf", 1), ("xf", 2), ("xf", 3), ("xf", 4), ("xf", 5)),
        (("b", 4), ("c", 3), ("x", 0), ("c", 4)),
        (("c", 6), ("d", 6), ("c", 7), ("d", 7), ("e", 0)),
        (("d", 0), ("d", 1)),
    ),
    (
        (("xf", 6), ("xf", 7)),
        (("b", 5), ("c", 5), ("x", 1), ("c", 6), ("x", 2), ("b", 6), ("c", 7)),
        (("e", 1), ("e", 2), ("e", 3)),
        (("d", 2), ("d", 3)),
    ),
    (
        (),
        (("x", 3), ("x", 4), ("b", 7), ("x", 5)),
        (("e", 4), ("e", 5), ("e", 6)),
        (("d", 4), ("d", 5), ("d", 6), ("d", 7)),
    ),
    (
        (("c", 0), ("c", 1), ("c", 2), ("c", 3), ("c", 4), ("c", 5), ("d", 0), ("d", 1), ("c", 6), ("d", 2), ("d", 3), ("d", 4), ("d", 5), ("d", 6), ("x", 0), ("x", 1), ("x", 2), ("c", 7), ("d", 7), ("x", 3), ("x", 4), ("x", 5), ("x", 6), ("x", 7)),
        (("x", 6), ("e", 0), ("e", 1), ("x", 7), ("e", 2), ("e", 3), ("e", 4), ("e", 5), ("e", 6), ("e", 7)),
        (("x", 0), ("e", 7), ("x", 1), ("x", 2), ("x", 3), ("x", 4), ("x", 5), ("x", 6), ("x", 7)),
        (),
    ),
)


def pieces(low, high):
    return [(a, min(STEP, high - a)) for a in range(low, high, STEP)]


def kernel(
    counts, x_hbm, top_hbm, vg_hbm, w_hbm, g_hbm,
    out, owned,
    x, top, vg, w, g, br, nm, mk, ga, gx, gp, msg, rm, rp,
    pk, zs, zr, ys, yr, half, rolled, scales, means,
    lsem, ms, mr, ps, pr, xs, xr, zss, zrs, yss, yrs, hs, hr, hello,
):
    dp = lax.axis_index("dp")
    sec = lax.axis_index("section")
    core = lax.rem(dp, 2)
    yy = lax.rem(lax.div(dp, 2), NY)
    zz = lax.div(dp, 2 * NY)

    def at(z, y, c):
        return (z * NY + y) * 2 + c

    behind = (dp, lax.rem(sec + 3, 4))
    ahead = (dp, lax.rem(sec + 1, 4))
    twin = (at(zz, yy, 1 - core), sec)
    lead = core == 0

    def on_y(d):
        return (at(zz, lax.rem(yy + d, NY), 0), sec)

    def on_z(d):
        return (at(lax.rem(zz + d, NZ), yy, 0), sec)

    loads = [
        pltpu.make_async_copy(s, d, lsem.at[i])
        for i, (s, d) in enumerate(
            [(vg_hbm, vg), (w_hbm, w), (x_hbm, x), (g_hbm, g), (top_hbm, top)]
        )
    ]
    for cp in loads:
        cp.start()
    barrier = pltpu.get_barrier_semaphore()
    def signal(sem, peer):
        pl.semaphore_signal(sem, inc=1, device_id=peer, device_id_type=MESH_ID)

    signal(barrier, behind)
    signal(barrier, ahead)

    @pl.when(lead)
    def _():
        signal(barrier, twin)
        for d in range(1, NY):
            pl.when(yy + d < NY)(lambda d=d: signal(barrier, on_y(d)))
        for d in range(1, NZ):
            pl.when(zz + d < NZ)(lambda d=d: signal(barrier, on_z(d)))

    def remote(src, dst, ssem, rsem, peer):
        return pltpu.make_async_remote_copy(
            src_ref=src, dst_ref=dst, send_sem=ssem, recv_sem=rsem,
            device_id=peer, device_id_type=MESH_ID,
        )

    def rows(k):
        return pl.ds(pl.multiple_of(k * SLOTS, SLOTS), SLOTS)

    def part(low, high):
        return pl.ds(low, high - low)

    def minus_c(k):
        here = (rows(k), part(0, C1))
        return remote(out.at[here], rm.at[here], ms.at[0, k], mr.at[0, k], behind)

    def minus_d(k):
        here = (rows(k), part(C1, C2))
        return remote(out.at[here], rm.at[here], ms.at[2, k], mr.at[2, k], behind)

    def minus_x(k):
        here = (rows(k), part(C2, WIDTH))
        return remote(msg.at[here], rm.at[here], ms.at[1, k], mr.at[1, k], behind)

    def plus_d(k):
        here = (rows(k), part(C1, C2))
        return remote(msg.at[here], rp.at[here], ps.at[0, k], pr.at[0, k], ahead)

    def plus_x(k, src):
        here = (rows(k), part(C2, WIDTH))
        return remote(src.at[here], rp.at[here], ps.at[1, k], pr.at[1, k], ahead)

    loads[0].wait()
    slot = lax.broadcasted_iota(jnp.int32, (SLOTS, VAL), 0)
    for m in range(MICRO):
        here = pl.ds(m * SLOTS, SLOTS)
        value = vg[here, :].astype(F32)
        mk[here, :] = jnp.where(slot < counts[0, m], value, 0.0).astype(BF16)
    loads[1].wait()
    for a in range(0, WIDTH, 1024):
        br[:, a : a + 1024] = lax.dot_general(
            mk[0:ROWS, :], w[a : a + 1024, :], (((1,), (1,)), ((), ())),
            preferred_element_type=F32,
        )
    loads[2].wait()
    loads[3].wait()
    loads[4].wait()
    ga[...] = jnp.zeros_like(ga)
    pl.semaphore_wait(barrier, jnp.where(lead, 2 + yy + zz, 3))

    @pl.when(lead)
    def _():
        for d in range(1, NY):
            pl.when(yy + d >= NY)(lambda d=d: signal(hello.at[0], on_y(d)))
        for d in range(1, NZ):
            pl.when(zz + d >= NZ)(lambda d=d: signal(hello.at[1], on_z(d)))

    def swap_rows(k):
        there = pl.ds(pl.multiple_of(ROWS + k * SLOTS, SLOTS), SLOTS)
        return remote(nm.at[rows(k)], nm.at[there], xs.at[k], xr.at[k], twin)


    def first(k, carry):
        r = rows(k)
        square = jnp.zeros((SLOTS, 128), F32)
        cross = jnp.zeros((SLOTS, 128), F32)
        for a, n in pieces(0, WIDTH):
            xa = x[r, a : a + n].astype(F32)
            gb = g[0:1, a : a + n] * br[r, a : a + n]
            s2, c2 = xa * xa, xa * gb
            for j in range(0, n, 128):
                square = square + s2[:, j : j + 128]
                cross = cross + c2[:, j : j + 128]
        scale = lax.rsqrt(jnp.sum(square, axis=1, keepdims=True) * (1.0 / WIDTH) + EPS)
        mean = jnp.sum(cross, axis=1, keepdims=True) * scale * (1.0 / WIDTH)
        scales[r, :] = jnp.broadcast_to(scale, (SLOTS, 128))
        means[r, :] = jnp.broadcast_to(mean, (SLOTS, 128))
        for a, n in pieces(0, WIDTH):
            cols = slice(a, a + n)
            unit = x[r, cols].astype(F32) * scale
            nm[r, cols] = (unit * g[0:1, cols]).astype(BF16)
            prod = unit * br[r, cols]
            ga[:, cols] += prod[0:8] + prod[8:16]
        pl.when(core == 1)(lambda: swap_rows(k).start())
        return carry

    lax.fori_loop(0, MICRO, first, 0)

    for j in range(WIDTH // 128):
        gx[j : j + 1, :] = jnp.sum(ga[:, j * 128 : j * 128 + 128], axis=0, keepdims=True)
    swaps = [
        remote(mk.at[pl.ds(0, ROWS)], mk.at[pl.ds(ROWS, ROWS)], xs.at[8], xr.at[8], twin),
        remote(gx, gp, xs.at[9], xr.at[9], twin),
    ]

    @pl.when(core == 1)
    def _():
        for cp in swaps:
            cp.start()

    def second(k, carry):
        r = rows(k)
        scale, mean = scales[r, 0:1], means[r, 0:1]
        for a, n in pieces(0, WIDTH):
            cols = slice(a, a + n)
            unit = x[r, cols].astype(F32) * scale
            br[r, cols] = scale * (g[0:1, cols] * br[r, cols] - unit * mean)

        @pl.when(sec == 3)
        def _():
            for a, n in pieces(0, WIDTH):
                cols = slice(a, a + n)
                out[r, cols] = (top[r, cols].astype(F32) + br[r, cols]).astype(BF16)
            minus_c(k).start()

        @pl.when(sec == 1)
        def _():
            for a, n in pieces(C1, WIDTH):
                msg[r, a : a + n] = br[r, a : a + n].astype(BF16)
            plus_d(k).start()

        @pl.when(sec == 2)
        def _():
            for a, n in pieces(C2, WIDTH):
                msg[r, a : a + n] = br[r, a : a + n].astype(BF16)
            plus_x(k, msg).start()

        return carry

    lax.fori_loop(0, MICRO, second, 0)

    @pl.when(sec == 3)
    def _():
        for k in range(MICRO):
            minus_d(k).start()

    def node3_d(k):
        plus_d(k).wait_recv()
        r = rows(k)
        for a, n in pieces(C1, C2):
            msg[r, a : a + n] = (rp[r, a : a + n].astype(F32) + br[r, a : a + n]).astype(BF16)
        plus_d(k).start()

    def node3_x(k):
        plus_x(k, msg).wait_recv()
        r = rows(k)
        for a, n in pieces(C2, WIDTH):
            msg[r, a : a + n] = (rp[r, a : a + n].astype(F32) + br[r, a : a + n]).astype(BF16)
        plus_x(k, msg).start()

    def add_minus(k, low, high):
        r = rows(k)
        for a, n in pieces(low, high):
            out[r, a : a + n] = (rm[r, a : a + n].astype(F32) + br[r, a : a + n]).astype(BF16)

    def relay_c(k):
        minus_c(k).wait_recv()
        add_minus(k, 0, C1)
        minus_c(k).start()

    def node2_e(k):
        minus_d(k).wait_recv()
        add_minus(k, C1, C2)
        minus_d(k).start()

    def node2_x(k):
        plus_x(k, msg).wait_recv()
        r = rows(k)
        for a, n in pieces(C2, WIDTH):
            out[r, a : a + n] = (
                top[r, a : a + n].astype(F32) + rp[r, a : a + n].astype(F32)
            ).astype(BF16)

    def node1_e(k):
        minus_d(k).wait_recv()
        add_minus(k, C1, C2)

    def node1_b(k):
        minus_x(k).start()

    def node1_x(k):
        plus_x(k, rp).wait_recv()
        plus_x(k, rp).start()
        r = rows(k)
        for a, n in pieces(C2, WIDTH):
            total = top[r, a : a + n].astype(F32) + rp[r, a : a + n].astype(F32)
            out[r, a : a + n] = (total + br[r, a : a + n]).astype(BF16)

    def node0_x_forward(k):
        plus_x(k, rp).wait_recv()
        plus_x(k, rp).start()

    def node0_x(k):
        minus_x(k).wait_recv()
        r = rows(k)
        for a, n in pieces(C2, WIDTH):
            total = top[r, a : a + n].astype(F32) + rp[r, a : a + n].astype(F32)
            total = total + rm[r, a : a + n].astype(F32)
            out[r, a : a + n] = (total + br[r, a : a + n]).astype(BF16)

    def node0_d(k):
        plus_d(k).wait_recv()
        r = rows(k)
        for a, n in pieces(C1, C2):
            total = top[r, a : a + n].astype(F32) + rp[r, a : a + n].astype(F32)
            out[r, a : a + n] = (total + br[r, a : a + n]).astype(BF16)

    def node0_c(k):
        minus_c(k).wait_recv()
        add_minus(k, 0, C1)

    steps = (
        {"xf": node0_x_forward, "x": node0_x, "d": node0_d, "c": node0_c},
        {"b": node1_b, "c": relay_c, "e": node1_e, "x": node1_x},
        {"c": relay_c, "d": node3_d, "e": node2_e, "x": node2_x},
        {"x": node3_x, "d": node3_d},
    )

    def chain(stretch):
        for section in range(4):
            todo = ORDER[stretch][section]
            if not todo:
                continue

            @pl.when(sec == section)
            def _(section=section, todo=todo):
                for name, k in todo:
                    steps[section][name](k)

    def owner_rows(z, y):
        start = z * (NY * BLOCK) + y * BLOCK
        return jnp.concatenate([pk[pl.ds(start, HALF), :], pk[pl.ds(start + 21, HALF), :]], axis=0)

    def group_rows(group):
        return pl.ds(group[0] * PAIR, (group[1] - group[0]) * PAIR)

    def y_copy(d, i):
        there = group_rows(GROUPS[i])
        return remote(
            ys.at[lax.rem(yy + d, NY), there], yr.at[NY - d, there],
            yss.at[d, i], yrs.at[NY - d, i], on_y(d),
        )

    def z_copy(z):
        return remote(zs.at[z], zr.at[zz], zss.at[z], zrs.at[zz], (at(z, yy, 0), sec))

    def product():
        for k in range(MICRO):
            swap_rows(k).wait_recv()
        for cp in swaps:
            cp.wait_recv()
        pk[0:32, :] = gx[...] + gp[...]
        for a in range(0, WIDTH, 512):
            pk[32 + a : 32 + a + 512, :] = lax.dot_general(
                nm[:, a : a + 512], mk[...], (((0,), (0,)), ((), ())),
                preferred_element_type=F32,
            )
        pk[4128:4136, :] = jnp.zeros((8, 128), F32)
        pl.when(yy < NY - 1)(lambda: pl.semaphore_wait(hello.at[0], NY - 1 - yy))
        for i, group in enumerate(GROUPS):
            def pack(z, carry):
                for y in range(NY):
                    here = pl.ds(pl.multiple_of(z * PAIR, PAIR), PAIR)
                    ys[y, here, :] = owner_rows(z, y).astype(BF16)
                return carry

            lax.fori_loop(group[0], group[1], pack, 0)
            for d in (4, 3, 5, 2, 6, 1, 7):
                y_copy(d, i).start()

    def y_sum(i):
        low, high = GROUPS[i]
        for d in range(1, NY):
            y_copy(NY - d, i).wait_recv()

        def add(z, carry):
            here = pl.ds(pl.multiple_of(z * PAIR, PAIR), PAIR)
            total = owner_rows(z, yy)
            for d in range(1, NY):
                total = total + yr[d, here, :].astype(F32)
            half[z] = total
            zs[z] = total.astype(BF16)
            return carry

        lax.fori_loop(low, high, add, 0)
        if i == 0:
            zr[zz] = jnp.zeros((PAIR, 128), BF16)
            pl.when(zz < NZ - 1)(lambda: pl.semaphore_wait(hello.at[1], NZ - 1 - zz))
        for z in range(low, high):
            pl.when(zz != z)(lambda z=z: z_copy(z).start())

    def z_arrival(z):
        return remote(zs.at[z], zr.at[z], zss.at[z], zrs.at[z], (at(z, yy, 0), sec))

    give = remote(rolled.at[1], rolled.at[2], hs, hr, twin)
    factor = 1.0 / math.sqrt(ROWS * 2 * NY * NZ)

    def z_sum():
        for z in range(NZ):
            pl.when(zz != z)(lambda z=z: z_arrival(z).wait_recv())
        late, total = half[zz, HALF:PAIR], half[zz, 0:HALF]
        for z in range(NZ):
            late = late + zr[z, HALF:PAIR].astype(F32)
        rolled[1] = late * factor
        give.start()
        for z in range(NZ):
            total = total + zr[z, 0:HALF].astype(F32)
        total = total * factor
        for j in range(21):
            owned[0:1, j * 128 : j * 128 + 128] = total[j : j + 1, :]
        owned[0:1, 2688:2752] = total[21:22, 0:64]

    def twin_last():
        give.wait_recv()
        turned = pltpu.roll(rolled[2], 64, 1)
        rolled[0] = turned
        lane = lax.broadcasted_iota(jnp.int32, (22, 128), 1)
        mine = jnp.where(lane < 64, rolled[0, 0:22, :], rolled[0, 1:23, :])
        for j in range(21):
            owned[0:1, j * 128 : j * 128 + 128] = mine[j : j + 1, :]
        owned[0:1, 2688:2752] = mine[21:22, 0:64]

    chain(0)
    pl.when(lead)(product)
    for i in range(len(GROUPS)):
        chain(i + 1)
        pl.when(lead)(lambda i=i: y_sum(i))
    chain(len(GROUPS) + 1)
    pl.when(lead)(z_sum)
    pl.when(core == 1)(twin_last)

    @pl.when(lead)
    def _():
        for i in range(len(GROUPS)):
            for d in range(1, NY):
                y_copy(d, i).wait_send()
        for z in range(NZ):
            pl.when(zz != z)(lambda z=z: z_copy(z).wait_send())
        give.wait_send()

    @pl.when(core == 1)
    def _():
        for k in range(MICRO):
            swap_rows(k).wait_send()
        for cp in swaps:
            cp.wait_send()

    def drain(k, carry):
        @pl.when(sec >= 2)
        def _():
            minus_d(k).wait_send()

        @pl.when(sec == 1)
        def _():
            minus_x(k).wait_send()

        @pl.when(sec >= 1)
        def _():
            minus_c(k).wait_send()
            plus_d(k).wait_send()

        plus_x(k, msg).wait_send()
        return carry

    lax.fori_loop(0, MICRO, drain, 0)


def shards(layer_inputs, top_grad, value_grads, weights, norm_gains, counts):
    anywhere = pl.BlockSpec(memory_space=pltpu.HBM)
    local = pl.BlockSpec(memory_space=pltpu.VMEM)
    dma = pltpu.SemaphoreType.DMA
    wide = (ROWS, WIDTH)
    grads, owned = pl.pallas_call(
        kernel,
        out_shape=(
            jax.ShapeDtypeStruct(wide, BF16),
            jax.ShapeDtypeStruct((1, 2752), F32),
        ),
        in_specs=[pl.BlockSpec(memory_space=pltpu.SMEM)] + [anywhere] * 5,
        out_specs=(local, local),
        scratch_shapes=[
            pltpu.VMEM(wide, BF16),
            pltpu.VMEM(wide, BF16),
            pltpu.VMEM((ROWS, VAL), BF16),
            pltpu.VMEM((WIDTH, VAL), BF16),
            pltpu.VMEM((1, WIDTH), F32),
            pltpu.VMEM(wide, F32),
            pltpu.VMEM((2 * ROWS, WIDTH), BF16),
            pltpu.VMEM((2 * ROWS, VAL), BF16),
            pltpu.VMEM((8, WIDTH), F32),
            pltpu.VMEM((32, 128), F32),
            pltpu.VMEM((32, 128), F32),
            pltpu.VMEM(wide, BF16),
            pltpu.VMEM(wide, BF16),
            pltpu.VMEM(wide, BF16),
            pltpu.VMEM((4136, 128), F32),
            pltpu.VMEM((NZ, PAIR, 128), BF16),
            pltpu.VMEM((NZ, PAIR, 128), BF16),
            pltpu.VMEM((NY, NZ * PAIR, 128), BF16),
            pltpu.VMEM((NY, NZ * PAIR, 128), BF16),
            pltpu.VMEM((NZ, PAIR, 128), F32),
            pltpu.VMEM((3, HALF, 128), F32),
            pltpu.VMEM((ROWS, 128), F32),
            pltpu.VMEM((ROWS, 128), F32),
            dma((5,)),
            dma((3, MICRO)), dma((3, MICRO)), dma((2, MICRO)), dma((2, MICRO)),
            dma((10,)), dma((10,)),
            dma((NZ,)), dma((NZ,)),
            dma((NY, len(GROUPS))), dma((NY, len(GROUPS))),
            dma, dma,
            pltpu.SemaphoreType.REGULAR((2,)),
        ],
        compiler_params=pltpu.CompilerParams(
            collective_id=0, has_side_effects=True, vmem_limit_bytes=40 * 2**20
        ),
    )(
        *(
            pltpu.with_memory_space_constraint(v, pltpu.HBM)
            for v in (
                counts.reshape(1, MICRO), layer_inputs[0], top_grad, value_grads[0],
                weights[0], norm_gains,
            )
        )
    )
    return grads.reshape(1, ROWS, WIDTH), owned


def solution(mesh):
    placed = (
        P("section", "dp", None),
        P("dp", None),
        P("section", "dp", None),
        P("section", None, None),
        P("section", None),
        P("dp"),
    )
    return jax.shard_map(
        shards,
        mesh=mesh,
        in_specs=placed,
        out_specs=(P("section", "dp", None), P("section", "dp")),
        check_vma=False,
    )
```

```python
import math

import jax
import jax.numpy as jnp
from jax import lax
from jax.experimental import pallas as pl
from jax.experimental.pallas import tpu as pltpu
from jax.sharding import PartitionSpec as P

EPS = 1e-05
MESH_ID = pl.DeviceIdType.MESH
F32, BF16 = jnp.float32, jnp.bfloat16

ROWS, WIDTH, VAL = 128, 4096, 128
MICRO, SLOTS = 8, 16
NZ, NY = 12, 8
BLOCK = 43
HALF = 24
PAIR = 2 * HALF
GROUPS = ((0, 2), (2, 5), (5, 8), (8, 12))

C1, C2 = 11 * 128, 22 * 128
STEP = 512

ORDER = (
    (
        (),
        (("b", 0),),
        (),
        (),
    ),
    (
        (("xf", 0),),
        (("b", 1), ("b", 2), ("c", 0), ("b", 3), ("c", 1), ("c", 2)),
        (("c", 0), ("d", 0), ("c", 1), ("d", 1), ("c", 2), ("d", 2), ("c", 3), ("d", 3), ("c", 4), ("d", 4), ("c", 5), ("d", 5)),
        (("x", 0), ("x", 1), ("x", 2), ("x", 3), ("x", 4), ("x", 5), ("x", 6), ("x", 7)),
    ),
    (
        (("xf", 1), ("xf", 2), ("xf", 3), ("xf", 4), ("xf", 5)),
        (("b", 4), ("c", 3), ("x", 0), ("c", 4)),
        (("c", 6), ("d", 6), ("c", 7), ("d", 7), ("e", 0)),
        (("d", 0), ("d", 1)),
    ),
    (
        (("xf", 6), ("xf", 7)),
        (("b", 5), ("c", 5), ("x", 1), ("c", 6), ("x", 2), ("b", 6), ("c", 7)),
        (("e", 1), ("e", 2), ("e", 3)),
        (("d", 2), ("d", 3)),
    ),
    (
        (),
        (("x", 3), ("x", 4), ("b", 7), ("x", 5)),
        (("e", 4), ("e", 5), ("e", 6)),
        (("d", 4), ("d", 5), ("d", 6), ("d", 7)),
    ),
    (
        (("c", 0), ("c", 1), ("c", 2), ("c", 3), ("c", 4), ("c", 5), ("d", 0), ("d", 1), ("c", 6), ("d", 2), ("d", 3), ("d", 4), ("d", 5), ("d", 6), ("x", 0), ("x", 1), ("x", 2), ("c", 7), ("d", 7), ("x", 3), ("x", 4), ("x", 5), ("x", 6), ("x", 7)),
        (("x", 6), ("e", 0), ("e", 1), ("x", 7), ("e", 2), ("e", 3), ("e", 4), ("e", 5), ("e", 6), ("e", 7)),
        (("x", 0), ("e", 7), ("x", 1), ("x", 2), ("x", 3), ("x", 4), ("x", 5), ("x", 6), ("x", 7)),
        (),
    ),
)


def pieces(low, high):
    return [(a, min(STEP, high - a)) for a in range(low, high, STEP)]


def kernel(
    counts, x_hbm, top_hbm, vg_hbm, w_hbm, g_hbm,
    out, owned,
    x, top, vg, w, g, br, nm, mk, ga, gx, gp, msg, rm, rp,
    pk, zs, zr, ys, yr, half, rolled, scales, means,
    lsem, ms, mr, ps, pr, xs, xr, zss, zrs, yss, yrs, hs, hr, hello,
):
    dp = lax.axis_index("dp")
    sec = lax.axis_index("section")
    core = lax.rem(dp, 2)
    yy = lax.rem(lax.div(dp, 2), NY)
    zz = lax.div(dp, 2 * NY)

    def at(z, y, c):
        return (z * NY + y) * 2 + c

    behind = (dp, lax.rem(sec + 3, 4))
    ahead = (dp, lax.rem(sec + 1, 4))
    twin = (at(zz, yy, 1 - core), sec)
    lead = core == 0

    def on_y(d):
        return (at(zz, lax.rem(yy + d, NY), 0), sec)

    def on_z(d):
        return (at(lax.rem(zz + d, NZ), yy, 0), sec)

    loads = [
        pltpu.make_async_copy(s, d, lsem.at[i])
        for i, (s, d) in enumerate(
            [(vg_hbm, vg), (w_hbm, w), (x_hbm, x), (g_hbm, g), (top_hbm, top)]
        )
    ]
    for cp in loads:
        cp.start()
    barrier = pltpu.get_barrier_semaphore()
    def signal(sem, peer):
        pl.semaphore_signal(sem, inc=1, device_id=peer, device_id_type=MESH_ID)

    signal(barrier, behind)
    signal(barrier, ahead)

    @pl.when(lead)
    def _():
        signal(barrier, twin)
        for d in range(1, NY):
            pl.when(yy + d < NY)(lambda d=d: signal(barrier, on_y(d)))
        for d in range(1, NZ):
            pl.when(zz + d < NZ)(lambda d=d: signal(barrier, on_z(d)))

    def remote(src, dst, ssem, rsem, peer):
        return pltpu.make_async_remote_copy(
            src_ref=src, dst_ref=dst, send_sem=ssem, recv_sem=rsem,
            device_id=peer, device_id_type=MESH_ID,
        )

    def rows(k):
        return pl.ds(pl.multiple_of(k * SLOTS, SLOTS), SLOTS)

    def part(low, high):
        return pl.ds(low, high - low)

    def minus_c(k):
        here = (rows(k), part(0, C1))
        return remote(out.at[here], rm.at[here], ms.at[0, k], mr.at[0, k], behind)

    def minus_d(k):
        here = (rows(k), part(C1, C2))
        return remote(out.at[here], rm.at[here], ms.at[2, k], mr.at[2, k], behind)

    def minus_x(k):
        here = (rows(k), part(C2, WIDTH))
        return remote(msg.at[here], rm.at[here], ms.at[1, k], mr.at[1, k], behind)

    def plus_d(k):
        here = (rows(k), part(C1, C2))
        return remote(msg.at[here], rp.at[here], ps.at[0, k], pr.at[0, k], ahead)

    def plus_x(k, src):
        here = (rows(k), part(C2, WIDTH))
        return remote(src.at[here], rp.at[here], ps.at[1, k], pr.at[1, k], ahead)

    loads[0].wait()
    slot = lax.broadcasted_iota(jnp.int32, (SLOTS, VAL), 0)
    for m in range(MICRO):
        here = pl.ds(m * SLOTS, SLOTS)
        value = vg[here, :].astype(F32)
        mk[here, :] = jnp.where(slot < counts[0, m], value, 0.0).astype(BF16)
    loads[1].wait()
    for a in range(0, WIDTH, 1024):
        br[:, a : a + 1024] = lax.dot_general(
            mk[0:ROWS, :], w[a : a + 1024, :], (((1,), (1,)), ((), ())),
            preferred_element_type=F32,
        )
    loads[2].wait()
    loads[3].wait()
    loads[4].wait()
    ga[...] = jnp.zeros_like(ga)
    pl.semaphore_wait(barrier, jnp.where(lead, 2 + yy + zz, 3))

    @pl.when(lead)
    def _():
        for d in range(1, NY):
            pl.when(yy + d >= NY)(lambda d=d: signal(hello.at[0], on_y(d)))
        for d in range(1, NZ):
            pl.when(zz + d >= NZ)(lambda d=d: signal(hello.at[1], on_z(d)))

    def swap_rows(k):
        there = pl.ds(pl.multiple_of(ROWS + k * SLOTS, SLOTS), SLOTS)
        return remote(nm.at[rows(k)], nm.at[there], xs.at[k], xr.at[k], twin)


    def first(k, carry):
        r = rows(k)
        square = jnp.zeros((SLOTS, 128), F32)
        cross = jnp.zeros((SLOTS, 128), F32)
        for a, n in pieces(0, WIDTH):
            xa = x[r, a : a + n].astype(F32)
            gb = g[0:1, a : a + n] * br[r, a : a + n]
            s2, c2 = xa * xa, xa * gb
            for j in range(0, n, 128):
                square = square + s2[:, j : j + 128]
                cross = cross + c2[:, j : j + 128]
        scale = lax.rsqrt(jnp.sum(square, axis=1, keepdims=True) * (1.0 / WIDTH) + EPS)
        mean = jnp.sum(cross, axis=1, keepdims=True) * scale * (1.0 / WIDTH)
        scales[r, :] = jnp.broadcast_to(scale, (SLOTS, 128))
        means[r, :] = jnp.broadcast_to(mean, (SLOTS, 128))
        for a, n in pieces(0, WIDTH):
            cols = slice(a, a + n)
            unit = x[r, cols].astype(F32) * scale
            nm[r, cols] = (unit * g[0:1, cols]).astype(BF16)
            prod = unit * br[r, cols]
            ga[:, cols] += prod[0:8] + prod[8:16]
        pl.when(core == 1)(lambda: swap_rows(k).start())
        return carry

    lax.fori_loop(0, MICRO, first, 0)

    for j in range(WIDTH // 128):
        gx[j : j + 1, :] = jnp.sum(ga[:, j * 128 : j * 128 + 128], axis=0, keepdims=True)
    swaps = [
        remote(mk.at[pl.ds(0, ROWS)], mk.at[pl.ds(ROWS, ROWS)], xs.at[8], xr.at[8], twin),
        remote(gx, gp, xs.at[9], xr.at[9], twin),
    ]

    @pl.when(core == 1)
    def _():
        for cp in swaps:
            cp.start()

    def second(k, carry):
        r = rows(k)
        scale, mean = scales[r, 0:1], means[r, 0:1]
        for a, n in pieces(0, WIDTH):
            cols = slice(a, a + n)
            unit = x[r, cols].astype(F32) * scale
            br[r, cols] = scale * (g[0:1, cols] * br[r, cols] - unit * mean)

        @pl.when(sec == 3)
        def _():
            for a, n in pieces(0, WIDTH):
                cols = slice(a, a + n)
                out[r, cols] = (top[r, cols].astype(F32) + br[r, cols]).astype(BF16)
            minus_c(k).start()

        @pl.when(sec == 1)
        def _():
            for a, n in pieces(C1, WIDTH):
                msg[r, a : a + n] = br[r, a : a + n].astype(BF16)
            plus_d(k).start()

        @pl.when(sec == 2)
        def _():
            for a, n in pieces(C2, WIDTH):
                msg[r, a : a + n] = br[r, a : a + n].astype(BF16)
            plus_x(k, msg).start()

        return carry

    lax.fori_loop(0, MICRO, second, 0)

    @pl.when(sec == 3)
    def _():
        for k in range(MICRO):
            minus_d(k).start()

    def node3_d(k):
        plus_d(k).wait_recv()
        r = rows(k)
        for a, n in pieces(C1, C2):
            msg[r, a : a + n] = (rp[r, a : a + n].astype(F32) + br[r, a : a + n]).astype(BF16)
        plus_d(k).start()

    def node3_x(k):
        plus_x(k, msg).wait_recv()
        r = rows(k)
        for a, n in pieces(C2, WIDTH):
            msg[r, a : a + n] = (rp[r, a : a + n].astype(F32) + br[r, a : a + n]).astype(BF16)
        plus_x(k, msg).start()

    def add_minus(k, low, high):
        r = rows(k)
        for a, n in pieces(low, high):
            out[r, a : a + n] = (rm[r, a : a + n].astype(F32) + br[r, a : a + n]).astype(BF16)

    def relay_c(k):
        minus_c(k).wait_recv()
        add_minus(k, 0, C1)
        minus_c(k).start()

    def node2_e(k):
        minus_d(k).wait_recv()
        add_minus(k, C1, C2)
        minus_d(k).start()

    def node2_x(k):
        plus_x(k, msg).wait_recv()
        r = rows(k)
        for a, n in pieces(C2, WIDTH):
            out[r, a : a + n] = (
                top[r, a : a + n].astype(F32) + rp[r, a : a + n].astype(F32)
            ).astype(BF16)

    def node1_e(k):
        minus_d(k).wait_recv()
        add_minus(k, C1, C2)

    def node1_b(k):
        minus_x(k).start()

    def node1_x(k):
        plus_x(k, rp).wait_recv()
        plus_x(k, rp).start()
        r = rows(k)
        for a, n in pieces(C2, WIDTH):
            total = top[r, a : a + n].astype(F32) + rp[r, a : a + n].astype(F32)
            out[r, a : a + n] = (total + br[r, a : a + n]).astype(BF16)

    def node0_x_forward(k):
        plus_x(k, rp).wait_recv()
        plus_x(k, rp).start()

    def node0_x(k):
        minus_x(k).wait_recv()
        r = rows(k)
        for a, n in pieces(C2, WIDTH):
            total = top[r, a : a + n].astype(F32) + rp[r, a : a + n].astype(F32)
            total = total + rm[r, a : a + n].astype(F32)
            out[r, a : a + n] = (total + br[r, a : a + n]).astype(BF16)

    def node0_d(k):
        plus_d(k).wait_recv()
        r = rows(k)
        for a, n in pieces(C1, C2):
            total = top[r, a : a + n].astype(F32) + rp[r, a : a + n].astype(F32)
            out[r, a : a + n] = (total + br[r, a : a + n]).astype(BF16)

    def node0_c(k):
        minus_c(k).wait_recv()
        add_minus(k, 0, C1)

    steps = (
        {"xf": node0_x_forward, "x": node0_x, "d": node0_d, "c": node0_c},
        {"b": node1_b, "c": relay_c, "e": node1_e, "x": node1_x},
        {"c": relay_c, "d": node3_d, "e": node2_e, "x": node2_x},
        {"x": node3_x, "d": node3_d},
    )

    def chain(stretch):
        for section in range(4):
            todo = ORDER[stretch][section]
            if not todo:
                continue

            @pl.when(sec == section)
            def _(section=section, todo=todo):
                for name, k in todo:
                    steps[section][name](k)

    def owner_rows(z, y):
        start = z * (NY * BLOCK) + y * BLOCK
        return jnp.concatenate([pk[pl.ds(start, HALF), :], pk[pl.ds(start + 21, HALF), :]], axis=0)

    def group_rows(group):
        return pl.ds(group[0] * PAIR, (group[1] - group[0]) * PAIR)

    def y_copy(d, i):
        there = group_rows(GROUPS[i])
        return remote(
            ys.at[lax.rem(yy + d, NY), there], yr.at[NY - d, there],
            yss.at[d, i], yrs.at[NY - d, i], on_y(d),
        )

    def z_copy(z):
        return remote(zs.at[z], zr.at[zz], zss.at[z], zrs.at[zz], (at(z, yy, 0), sec))

    def product():
        for k in range(MICRO):
            swap_rows(k).wait_recv()
        for cp in swaps:
            cp.wait_recv()
        pk[0:32, :] = gx[...] + gp[...]
        for a in range(0, WIDTH, 512):
            pk[32 + a : 32 + a + 512, :] = lax.dot_general(
                nm[:, a : a + 512], mk[...], (((0,), (0,)), ((), ())),
                preferred_element_type=F32,
            )
        pk[4128:4136, :] = jnp.zeros((8, 128), F32)
        pl.when(yy < NY - 1)(lambda: pl.semaphore_wait(hello.at[0], NY - 1 - yy))
        for i, group in enumerate(GROUPS):
            def pack(z, carry):
                for y in range(NY):
                    here = pl.ds(pl.multiple_of(z * PAIR, PAIR), PAIR)
                    ys[y, here, :] = owner_rows(z, y).astype(BF16)
                return carry

            lax.fori_loop(group[0], group[1], pack, 0)
            for d in (4, 3, 5, 2, 6, 1, 7):
                y_copy(d, i).start()

    def y_sum(i):
        low, high = GROUPS[i]
        for d in range(1, NY):
            y_copy(NY - d, i).wait_recv()

        def add(z, carry):
            here = pl.ds(pl.multiple_of(z * PAIR, PAIR), PAIR)
            total = owner_rows(z, yy)
            for d in range(1, NY):
                total = total + yr[d, here, :].astype(F32)
            half[z] = total
            zs[z] = total.astype(BF16)
            return carry

        lax.fori_loop(low, high, add, 0)
        if i == 0:
            zr[zz] = jnp.zeros((PAIR, 128), BF16)
            pl.when(zz < NZ - 1)(lambda: pl.semaphore_wait(hello.at[1], NZ - 1 - zz))
        for z in range(low, high):
            pl.when(zz != z)(lambda z=z: z_copy(z).start())

    def z_arrival(z):
        return remote(zs.at[z], zr.at[z], zss.at[z], zrs.at[z], (at(z, yy, 0), sec))

    give = remote(rolled.at[1], rolled.at[2], hs, hr, twin)
    factor = 1.0 / math.sqrt(ROWS * 2 * NY * NZ)

    def z_sum():
        for z in range(NZ):
            pl.when(zz != z)(lambda z=z: z_arrival(z).wait_recv())
        late, total = half[zz, HALF:PAIR], half[zz, 0:HALF]
        for z in range(NZ):
            late = late + zr[z, HALF:PAIR].astype(F32)
        rolled[1] = late * factor
        give.start()
        for z in range(NZ):
            total = total + zr[z, 0:HALF].astype(F32)
        total = total * factor
        for j in range(21):
            owned[0:1, j * 128 : j * 128 + 128] = total[j : j + 1, :]
        owned[0:1, 2688:2752] = total[21:22, 0:64]

    def twin_last():
        give.wait_recv()
        turned = pltpu.roll(rolled[2], 64, 1)
        rolled[0] = turned
        lane = lax.broadcasted_iota(jnp.int32, (22, 128), 1)
        mine = jnp.where(lane < 64, rolled[0, 0:22, :], rolled[0, 1:23, :])
        for j in range(21):
            owned[0:1, j * 128 : j * 128 + 128] = mine[j : j + 1, :]
        owned[0:1, 2688:2752] = mine[21:22, 0:64]

    chain(0)
    pl.when(lead)(product)
    for i in range(len(GROUPS)):
        chain(i + 1)
        pl.when(lead)(lambda i=i: y_sum(i))
    late_start = lead & (sec == 0) & (dp == 0)
    pl.when(late_start)(z_sum)
    chain(len(GROUPS) + 1)
    pl.when(lead & jnp.logical_not(late_start))(z_sum)
    pl.when(core == 1)(twin_last)

    @pl.when(lead)
    def _():
        for i in range(len(GROUPS)):
            for d in range(1, NY):
                y_copy(d, i).wait_send()
        for z in range(NZ):
            pl.when(zz != z)(lambda z=z: z_copy(z).wait_send())
        give.wait_send()

    @pl.when(core == 1)
    def _():
        for k in range(MICRO):
            swap_rows(k).wait_send()
        for cp in swaps:
            cp.wait_send()

    def drain(k, carry):
        @pl.when(sec >= 2)
        def _():
            minus_d(k).wait_send()

        @pl.when(sec == 1)
        def _():
            minus_x(k).wait_send()

        @pl.when(sec >= 1)
        def _():
            minus_c(k).wait_send()
            plus_d(k).wait_send()

        plus_x(k, msg).wait_send()
        return carry

    lax.fori_loop(0, MICRO, drain, 0)


def shards(layer_inputs, top_grad, value_grads, weights, norm_gains, counts):
    anywhere = pl.BlockSpec(memory_space=pltpu.HBM)
    local = pl.BlockSpec(memory_space=pltpu.VMEM)
    dma = pltpu.SemaphoreType.DMA
    wide = (ROWS, WIDTH)
    grads, owned = pl.pallas_call(
        kernel,
        out_shape=(
            jax.ShapeDtypeStruct(wide, BF16),
            jax.ShapeDtypeStruct((1, 2752), F32),
        ),
        in_specs=[pl.BlockSpec(memory_space=pltpu.SMEM)] + [anywhere] * 5,
        out_specs=(local, local),
        scratch_shapes=[
            pltpu.VMEM(wide, BF16),
            pltpu.VMEM(wide, BF16),
            pltpu.VMEM((ROWS, VAL), BF16),
            pltpu.VMEM((WIDTH, VAL), BF16),
            pltpu.VMEM((1, WIDTH), F32),
            pltpu.VMEM(wide, F32),
            pltpu.VMEM((2 * ROWS, WIDTH), BF16),
            pltpu.VMEM((2 * ROWS, VAL), BF16),
            pltpu.VMEM((8, WIDTH), F32),
            pltpu.VMEM((32, 128), F32),
            pltpu.VMEM((32, 128), F32),
            pltpu.VMEM(wide, BF16),
            pltpu.VMEM(wide, BF16),
            pltpu.VMEM(wide, BF16),
            pltpu.VMEM((4136, 128), F32),
            pltpu.VMEM((NZ, PAIR, 128), BF16),
            pltpu.VMEM((NZ, PAIR, 128), BF16),
            pltpu.VMEM((NY, NZ * PAIR, 128), BF16),
            pltpu.VMEM((NY, NZ * PAIR, 128), BF16),
            pltpu.VMEM((NZ, PAIR, 128), F32),
            pltpu.VMEM((3, HALF, 128), F32),
            pltpu.VMEM((ROWS, 128), F32),
            pltpu.VMEM((ROWS, 128), F32),
            dma((5,)),
            dma((3, MICRO)), dma((3, MICRO)), dma((2, MICRO)), dma((2, MICRO)),
            dma((10,)), dma((10,)),
            dma((NZ,)), dma((NZ,)),
            dma((NY, len(GROUPS))), dma((NY, len(GROUPS))),
            dma, dma,
            pltpu.SemaphoreType.REGULAR((2,)),
        ],
        compiler_params=pltpu.CompilerParams(
            collective_id=0, has_side_effects=True, vmem_limit_bytes=40 * 2**20
        ),
    )(
        *(
            pltpu.with_memory_space_constraint(v, pltpu.HBM)
            for v in (
                counts.reshape(1, MICRO), layer_inputs[0], top_grad, value_grads[0],
                weights[0], norm_gains,
            )
        )
    )
    return grads.reshape(1, ROWS, WIDTH), owned


def solution(mesh):
    placed = (
        P("section", "dp", None),
        P("dp", None),
        P("section", "dp", None),
        P("section", None, None),
        P("section", None),
        P("dp"),
    )
    return jax.shard_map(
        shards,
        mesh=mesh,
        in_specs=placed,
        out_specs=(P("section", "dp", None), P("section", "dp")),
        check_vma=False,
    )
```
